32 devices in a mesh: sector: 8 (over z, y), mpo: 4 (over x, core).
Axes of the slice: x: 2, y: 2, z: 4, core: 2. Of those that a mesh axis runs over, the one named last changes fastest.
Arguments:
- vectors: bfloat16 [16, 8, 256, 256], P(None, 'sector'), may hold values from -6 to 6
- left_env: bfloat16 [16, 8, 256, 256], P('mpo', 'sector'), may hold values from -4 to 4
- right_env: bfloat16 [16, 8, 256, 256], P('mpo', 'sector'), may hold values from -4 to 4
- bond_shift: int32 [16], replicated, may hold values from -1 to 1, as said below
Outputs:
- sigma: bfloat16 [16, 8, 256, 256], P('mpo', 'sector')
- intersection: float32 [16, 16], replicated
- ham_small: float32 [16, 16], replicated
The draws below stay inside these ranges and needn't reach their ends.
Inputs may be any that keep to these rules, and one draw needn't show every extreme that they name: `bond_shift`: every one of -1, 0 and 1 occurs.
All inputs are finite; a program needn't handle non-finite values.
Results may differ from the reference program's by a relative error of at most 0.0034.
Values may be sent and summed in bfloat16 or wider, within the bound.
A program may use at most 128 MiB of HBM per device.

```python
import math
import jax
import jax.numpy as jnp
from jax import lax

BLK = 256
VECS = 16
NSEC = 8
BONDS = 16


def env_blocks(key):
    first = jax.random.fold_in(key, 0)
    index = jnp.arange(BLK, dtype=jnp.int32)
    band = 0.3 * (jnp.abs(index[:, None] - index[None, :]) == 1).astype(jnp.float32)
    noise = jax.random.truncated_normal(first, -4.0, 4.0, (BONDS, NSEC, BLK, BLK), jnp.float32) * (0.6 / BLK ** 0.5)
    diag = jnp.ones((BONDS, NSEC, BLK), jnp.float32)
    block = noise + band + diag[..., None] * jnp.eye(BLK, dtype=jnp.float32)
    return block * BONDS ** (-0.25)


def draw_left_env(key, part):
    return env_blocks(jax.random.fold_in(key, 11)).astype(jnp.bfloat16)


def draw_right_env(key, part):
    return env_blocks(jax.random.fold_in(key, 23)).astype(jnp.bfloat16)


def draw_vectors(key, part):
    keys = jax.random.split(jax.random.fold_in(key, 5), 4)
    places = jnp.arange(BLK, dtype=jnp.float32) / BLK
    phase = jax.random.uniform(keys[0], (4,), jnp.float32, 0.0, 2.0 * math.pi)
    first = jnp.cos(2.0 * math.pi * places + phase[0])[:, None] * jnp.cos(2.0 * math.pi * places + phase[1])[None, :]
    second = jnp.cos(4.0 * math.pi * places + phase[2])[:, None] * jnp.cos(6.0 * math.pi * places + phase[3])[None, :]
    weights = jax.random.uniform(keys[1], (VECS, 2), jnp.float32, 0.6, 1.2)
    sector_fac = jax.random.uniform(keys[2], (2, NSEC), jnp.float32, 0.8, 1.2)
    shared = weights[:, 0, None, None, None] * sector_fac[0][None, :, None, None] * first[None, None]
    shared = shared + weights[:, 1, None, None, None] * sector_fac[1][None, :, None, None] * second[None, None]
    noise = jax.random.truncated_normal(keys[3], -4.0, 4.0, (VECS, NSEC, BLK, BLK), jnp.float32)
    return (shared + 0.75 * noise).astype(jnp.bfloat16)


def draw_bond_shift(key, part):
    first, second = jax.random.split(jax.random.fold_in(key, 37))
    base = jax.random.randint(first, (BONDS,), -1, 2).astype(jnp.int32)
    order = jax.random.permutation(second, BONDS)
    base = base.at[order[:3]].set(jnp.array([-1, 0, 1], jnp.int32))
    return base.astype(jnp.int32)


def setup_inputs(seed: int = 0) -> dict:
    key_of = jax.random.split(jax.random.key(seed), 5)
    return {
        "vectors": draw_vectors(jax.random.fold_in(key_of[4], 71), 0),
        "left_env": draw_left_env(jax.random.fold_in(key_of[4], 71), 0),
        "right_env": draw_right_env(jax.random.fold_in(key_of[4], 71), 0),
        "bond_shift": draw_bond_shift(jax.random.fold_in(key_of[4], 71), 0),
    }


def reference(vectors, left_env, right_env, bond_shift):
    padded = jnp.pad(vectors, ((0, 0), (1, 1), (0, 0), (0, 0)))
    count = vectors.shape[1]

    def bond_step(total, items):
        lenv, renv, shift = items
        start = (1 + shift).astype(jnp.int32)
        source = lax.dynamic_slice_in_dim(padded, start, count, 1)
        left = jnp.einsum('sab,vsbc->vsac', lenv.astype(jnp.float32), source.astype(jnp.float32)).astype(jnp.bfloat16)
        term = jnp.einsum('vsac,scd->vsad', left.astype(jnp.float32), renv.astype(jnp.float32))
        return total + term, None

    zeros = jnp.zeros(vectors.shape, jnp.float32)
    total, _ = lax.scan(bond_step, zeros, (left_env, right_env, bond_shift))
    sigma = total.astype(jnp.bfloat16)
    scale = 1.0 / (vectors.shape[1] * vectors.shape[2] * vectors.shape[3])
    vf = vectors.astype(jnp.float32)
    intersection = jnp.einsum('isab,jsab->ij', vf, vf) * scale
    ham_small = jnp.einsum('isab,jsab->ij', vf, sigma.astype(jnp.float32)) * scale
    return sigma, intersection, ham_small
```

```python
import functools

import jax
import jax.numpy as jnp
from jax import lax
from jax.experimental import pallas as pl
from jax.experimental.pallas import tpu as pltpu
from jax.sharding import PartitionSpec as P

MESH = pl.DeviceIdType.MESH
F32 = jnp.float32
BF16 = jnp.bfloat16


def dot(a, b):
    return jnp.dot(a, b, preferred_element_type=F32)


def gram_row(vall, cols, first, nv, per):
    rows = vall.shape[1]
    blk = vall.shape[2]
    prod = jnp.zeros((per * nv, nv * nv), F32)
    for r in range(rows // nv):
        x = vall[:, r * nv : (r + 1) * nv, :].reshape(nv * nv, blk)
        y = cols[:, r * nv : (r + 1) * nv, :].reshape(per * nv, blk)
        prod += lax.dot_general(y, x, (((1,), (1,)), ((), ())), preferred_element_type=F32)
    sub = lax.broadcasted_iota(jnp.int32, prod.shape, 0) % nv
    lane = lax.broadcasted_iota(jnp.int32, prod.shape, 1) % nv
    prod = jnp.where(sub == lane, prod, 0.0)
    summed = jnp.concatenate(
        [jnp.sum(prod[j * nv : (j + 1) * nv], axis=0, keepdims=True) for j in range(per)], axis=0
    )
    width = nv * nv
    place = lax.broadcasted_iota(jnp.int32, summed.shape, 1) % nv
    step = 1
    while step < nv:
        up = pltpu.roll(summed, step, 1)
        down = pltpu.roll(summed, width - step, 1)
        summed = summed + jnp.where((place // step) % 2 == 1, up, down)
        step *= 2
    which = lax.broadcasted_iota(jnp.int32, summed.shape, 0)
    return jnp.sum(jnp.where(place == first + which, summed, 0.0), axis=0, keepdims=True)


def kernel(n_sec, n_mpo, nv, per, nb, scale, vec, left, right, shift, sigma, inter, ham, *scratch):
    ext = scratch[:per]
    (
        env_l, env_r, vall, acc, row_i, row_h, all_i, all_h,
        loc_sem, pair_s, pair_r, fwd_s, fwd_r, x_s, x_r, die_s, die_r,
        small_s, small_r,
    ) = scratch[per:]
    chips = n_mpo // 2
    total = n_sec * n_mpo
    sec = lax.axis_index("sector")
    mpo = lax.axis_index("mpo")
    me = sec * n_mpo + mpo
    core = mpo % 2
    chip = mpo // 2
    partner = chip * 2 + (1 - core)

    barrier = pltpu.get_barrier_semaphore()

    def greet(k, carry):
        other = (me + k) % total
        pl.semaphore_signal(
            barrier, inc=1, device_id=(other // n_mpo, other % n_mpo), device_id_type=MESH
        )
        return carry

    lax.fori_loop(1, total, greet, 0)
    pl.semaphore_wait(barrier, total - 1)

    par = sec % 2
    pair = sec + 1 - 2 * par
    slot_pair = 2 - 2 * par
    slot_fwd = 2 * par
    ahead = sec + 2 * (1 - 2 * par)
    behind = sec - 2 * (1 - 2 * par)
    has_ahead = (ahead >= 0) & (ahead < n_sec)
    has_behind = (behind >= 0) & (behind < n_sec)

    def remote(src, dst, send, recv, target):
        return pltpu.make_async_remote_copy(
            src_ref=src, dst_ref=dst, send_sem=send, recv_sem=recv,
            device_id=target, device_id_type=MESH,
        )

    def x_copies(d, k):
        target = (sec, ((chip + d) % chips) * 2 + core)
        slot = 2 * d
        return (
            remote(left.at[k, 0], env_l.at[slot, k], x_s.at[d, 0, k], x_r.at[d, 0, k], target),
            remote(right.at[k, 0], env_r.at[slot, k], x_s.at[d, 1, k], x_r.at[d, 1, k], target),
        )

    def die_copies(d, k):
        target = (sec, partner)
        src_l = left.at[k, 0] if d == 0 else env_l.at[2 * d, k]
        src_r = right.at[k, 0] if d == 0 else env_r.at[2 * d, k]
        return (
            remote(src_l, env_l.at[2 * d + 1, k], die_s.at[d, 0, k], die_r.at[d, 0, k], target),
            remote(src_r, env_r.at[2 * d + 1, k], die_s.at[d, 1, k], die_r.at[d, 1, k], target),
        )

    def pair_copy(v):
        return remote(
            vec.at[mpo * per + v, 0], ext[v].at[slot_fwd], pair_s.at[v], pair_r.at[v], (pair, mpo)
        )

    def fwd_copy(v):
        return remote(
            ext[v].at[slot_pair], ext[v].at[slot_fwd], fwd_s.at[v], fwd_r.at[v], (ahead, mpo)
        )

    for k in range(nb):
        for d in range(1, chips):
            for c in x_copies(d, k):
                c.start()
        if k < per:
            pair_copy(k).start()
    for v in range(nb, per):
        pair_copy(v).start()
    local = [
        pltpu.make_async_copy(left.at[:, 0], env_l.at[0], loc_sem.at[0]),
        pltpu.make_async_copy(right.at[:, 0], env_r.at[0], loc_sem.at[1]),
        pltpu.make_async_copy(vec.at[:, 0], vall, loc_sem.at[2]),
    ] + [
        pltpu.make_async_copy(vec.at[mpo * per + v, 0], ext[v].at[1], loc_sem.at[3 + v])
        for v in range(per)
    ]
    for c in local:
        c.start()
    for k in range(nb):
        for c in die_copies(0, k):
            c.start()

    @pl.when(jnp.logical_not(has_behind))
    def _():
        for v in range(per):
            ext[v][slot_fwd] = jnp.zeros(ext[v].shape[1:], BF16)

    acc[...] = jnp.zeros_like(acc)
    for c in local:
        c.wait()

    def share(row, rows, which):
        rows[me] = row[...]

        def send(k, carry):
            other = (me + k) % total
            remote(
                row, rows.at[me], small_s.at[which], small_r.at[which],
                (other // n_mpo, other % n_mpo),
            ).start()
            return carry

        lax.fori_loop(1, total, send, 0)

    def collect(rows, out, which):
        most = rows.at[pl.ds(0, total - 1)]
        pltpu.make_async_copy(most, most, small_s.at[which]).wait()
        pltpu.make_async_copy(most, most, small_r.at[which]).wait()

        def add(k, carry):
            return carry + rows[k]

        line = lax.fori_loop(0, total, add, jnp.zeros(rows.shape[1:], F32)) * scale
        for i in range(nv):
            out[i : i + 1, :] = line[:, i * nv : (i + 1) * nv]

    def forward(v):
        pair_copy(v).wait_recv()

        @pl.when(has_ahead)
        def _():
            fwd_copy(v).start()

    def bond(slot, k):
        d = slot // 2
        from_chip = (chip + chips - d) % chips
        from_core = (core + slot % 2) % 2
        return (from_chip * 2 + from_core) * nb + k

    def near_terms(v):
        @pl.when(has_behind)
        def _():
            fwd_copy(v).wait_recv()

        def step(it, carry):
            slot = it // nb
            k = it % nb
            src = ext[v][1 + shift[bond(slot, k)]]
            mid = dot(env_l[slot, k], src).astype(BF16)
            acc[v] += dot(mid, env_r[slot, k])
            return carry

        lax.fori_loop(0, 2 * nb, step, 0)

    def far_term(slot, k):
        sh = 1 + shift[bond(slot, k)]
        lhs = env_l[slot, k]
        rhs = env_r[slot, k]
        for v in range(per):
            acc[v] += dot(dot(lhs, ext[v][sh]).astype(BF16), rhs)

    forward(0)
    own = jnp.stack([ext[v][1] for v in range(per)], axis=0)
    row_i[...] = gram_row(vall, own, mpo * per, nv, per)
    share(row_i, all_i, 0)
    for k in range(nb):
        for c in die_copies(0, k):
            c.wait_recv()
    for v in range(per):
        if v + 1 < per:
            forward(v + 1)
        near_terms(v)

    for d in range(1, chips):

        def arrive(k, carry):
            for c in x_copies(d, k):
                c.wait_recv()
            for c in die_copies(d, k):
                c.start()
            far_term(2 * d, k)
            for c in die_copies(d, k):
                c.wait_recv()
            far_term(2 * d + 1, k)
            return carry

        lax.fori_loop(0, nb, arrive, 0)

    sigma[:, 0] = acc[...].astype(BF16)
    row_h[...] = gram_row(vall, sigma[:, 0], mpo * per, nv, per)
    share(row_h, all_h, 1)
    collect(all_i, inter, 0)

    for k in range(nb):
        for d in range(chips):
            for c in die_copies(d, k):
                c.wait_send()
            if d:
                for c in x_copies(d, k):
                    c.wait_send()
    for v in range(per):
        pair_copy(v).wait_send()

    @pl.when(has_ahead)
    def _():
        for v in range(per):
            fwd_copy(v).wait_send()

    collect(all_h, ham, 1)


def body(vectors, left_env, right_env, bond_shift):
    n_sec = lax.axis_size("sector")
    n_mpo = lax.axis_size("mpo")
    nv, _, rows, blk = vectors.shape
    nb = left_env.shape[0]
    per = nv // n_mpo
    total = n_sec * n_mpo
    chips = n_mpo // 2
    scale = 1.0 / (n_sec * vectors.shape[1] * rows * blk)
    any_spec = pl.BlockSpec(memory_space=pl.ANY)
    vmem_spec = pl.BlockSpec(memory_space=pltpu.VMEM)
    dma = pltpu.SemaphoreType.DMA
    return pl.pallas_call(
        functools.partial(kernel, n_sec, n_mpo, nv, per, nb, scale),
        out_shape=(
            jax.ShapeDtypeStruct((per, 1, rows, blk), BF16),
            jax.ShapeDtypeStruct((nv, nv), F32),
            jax.ShapeDtypeStruct((nv, nv), F32),
        ),
        in_specs=[any_spec] * 3 + [pl.BlockSpec(memory_space=pltpu.SMEM)],
        out_specs=(vmem_spec,) * 3,
        scratch_shapes=[pltpu.VMEM((3, rows, blk), BF16) for _ in range(per)]
        + [
            pltpu.VMEM((n_mpo, nb, rows, rows), BF16),
            pltpu.VMEM((n_mpo, nb, blk, blk), BF16),
            pltpu.VMEM((nv, rows, blk), BF16),
            pltpu.VMEM((per, rows, blk), F32),
            pltpu.VMEM((1, nv * nv), F32),
            pltpu.VMEM((1, nv * nv), F32),
            pltpu.VMEM((total, 1, nv * nv), F32),
            pltpu.VMEM((total, 1, nv * nv), F32),
            dma((3 + per,)),
            dma((per,)), dma((per,)), dma((per,)), dma((per,)),
            dma((chips, 2, nb)), dma((chips, 2, nb)),
            dma((chips, 2, nb)), dma((chips, 2, nb)),
            dma((2,)), dma((2,)),
        ],
        compiler_params=pltpu.CompilerParams(
            collective_id=0, has_side_effects=True, vmem_limit_bytes=48 << 20
        ),
        name="davidson",
    )(vectors, left_env, right_env, bond_shift)


def solution(mesh):
    return jax.shard_map(
        body,
        mesh=mesh,
        in_specs=(
            P(None, "sector", None, None),
            P("mpo", "sector", None, None),
            P("mpo", "sector", None, None),
            P(),
        ),
        out_specs=(P("mpo", "sector", None, None), P(), P()),
        check_vma=False,
    )
```

```python
import functools

import jax
import jax.numpy as jnp
from jax import lax
from jax.experimental import pallas as pl
from jax.experimental.pallas import tpu as pltpu
from jax.sharding import PartitionSpec as P

MESH = pl.DeviceIdType.MESH
F32 = jnp.float32
BF16 = jnp.bfloat16


def dot(a, b):
    return jnp.dot(a, b, preferred_element_type=F32)


def gram_row(vall, cols, first, nv, per):
    rows = vall.shape[1]
    blk = vall.shape[2]
    prod = jnp.zeros((per * nv, nv * nv), F32)
    for r in range(rows // nv):
        x = vall[:, r * nv : (r + 1) * nv, :].reshape(nv * nv, blk)
        y = cols[:, r * nv : (r + 1) * nv, :].reshape(per * nv, blk)
        prod += lax.dot_general(y, x, (((1,), (1,)), ((), ())), preferred_element_type=F32)
    sub = lax.broadcasted_iota(jnp.int32, prod.shape, 0) % nv
    lane = lax.broadcasted_iota(jnp.int32, prod.shape, 1) % nv
    prod = jnp.where(sub == lane, prod, 0.0)
    summed = jnp.concatenate(
        [jnp.sum(prod[j * nv : (j + 1) * nv], axis=0, keepdims=True) for j in range(per)], axis=0
    )
    width = nv * nv
    place = lax.broadcasted_iota(jnp.int32, summed.shape, 1) % nv
    step = 1
    while step < nv:
        up = pltpu.roll(summed, step, 1)
        down = pltpu.roll(summed, width - step, 1)
        summed = summed + jnp.where((place // step) % 2 == 1, up, down)
        step *= 2
    which = lax.broadcasted_iota(jnp.int32, summed.shape, 0)
    return jnp.sum(jnp.where(place == first + which, summed, 0.0), axis=0, keepdims=True)


def kernel(n_sec, n_mpo, nv, per, nb, scale, vec, left, right, shift, sigma, inter, ham, *scratch):
    ext = scratch[:per]
    (
        env_l, env_r, vall, acc, row_i, row_h, all_i, all_h,
        loc_sem, pair_s, pair_r, fwd_s, fwd_r, x_s, x_r, die_s, die_r,
        small_s, small_r, token,
    ) = scratch[per:]
    chips = n_mpo // 2
    total = n_sec * n_mpo
    sec = lax.axis_index("sector")
    mpo = lax.axis_index("mpo")
    me = sec * n_mpo + mpo
    core = mpo % 2
    chip = mpo // 2
    partner = chip * 2 + (1 - core)

    par = sec % 2
    pair = sec + 1 - 2 * par
    slot_pair = 2 - 2 * par
    slot_fwd = 2 * par
    ahead = sec + 2 * (1 - 2 * par)
    behind = sec - 2 * (1 - 2 * par)
    has_ahead = (ahead >= 0) & (ahead < n_sec)
    has_behind = (behind >= 0) & (behind < n_sec)

    barrier = pltpu.get_barrier_semaphore()

    def greet(target):
        pl.semaphore_signal(barrier, inc=1, device_id=target, device_id_type=MESH)

    for d in range(1, n_mpo):
        greet((sec, (mpo + d) % n_mpo))
    for d in range(n_mpo):
        greet((pair, (mpo + d) % n_mpo))

    @pl.when(has_ahead)
    def _():
        greet((ahead, mpo))

    @pl.when(has_behind)
    def _():
        greet((behind, mpo))

    pl.semaphore_wait(
        barrier, 2 * n_mpo - 1 + has_ahead.astype(jnp.int32) + has_behind.astype(jnp.int32)
    )

    def pass_tokens():
        @pl.when(has_behind)
        def _():
            pl.semaphore_wait(token.at[0], 1)

        @pl.when(has_ahead)
        def _():
            pl.semaphore_signal(token.at[0], inc=1, device_id=(ahead, mpo), device_id_type=MESH)
            pl.semaphore_wait(token.at[1], 1)

        @pl.when(has_behind)
        def _():
            pl.semaphore_signal(token.at[1], inc=1, device_id=(behind, mpo), device_id_type=MESH)

    def remote(src, dst, send, recv, target):
        return pltpu.make_async_remote_copy(
            src_ref=src, dst_ref=dst, send_sem=send, recv_sem=recv,
            device_id=target, device_id_type=MESH,
        )

    def x_copies(d, k):
        target = (sec, ((chip + d) % chips) * 2 + core)
        return (
            remote(left.at[k, 0], env_l.at[d, k, 0], x_s.at[d, 0, k], x_r.at[d, 0, k], target),
            remote(right.at[k, 0], env_r.at[d, k, 0], x_s.at[d, 1, k], x_r.at[d, 1, k], target),
        )

    def die_copies(d, k):
        target = (sec, partner)
        src_l = left.at[k, 0] if d == 0 else env_l.at[d, k, 0]
        src_r = right.at[k, 0] if d == 0 else env_r.at[d, k, 0]
        return (
            remote(src_l, env_l.at[d, k, 1], die_s.at[d, 0, k], die_r.at[d, 0, k], target),
            remote(src_r, env_r.at[d, k, 1], die_s.at[d, 1, k], die_r.at[d, 1, k], target),
        )

    def pair_copy(v):
        return remote(
            vec.at[mpo * per + v, 0], ext[v].at[slot_fwd], pair_s.at[v], pair_r.at[v], (pair, mpo)
        )

    def fwd_copy(v):
        return remote(
            ext[v].at[slot_pair], ext[v].at[slot_fwd], fwd_s.at[v], fwd_r.at[v], (ahead, mpo)
        )

    for k in range(nb):
        for d in range(1, chips):
            for c in x_copies(d, k):
                c.start()
        if k < per:
            pair_copy(k).start()
    for v in range(nb, per):
        pair_copy(v).start()
    local = [
        pltpu.make_async_copy(left.at[:, 0], env_l.at[0, :, 0], loc_sem.at[0]),
        pltpu.make_async_copy(right.at[:, 0], env_r.at[0, :, 0], loc_sem.at[1]),
        pltpu.make_async_copy(vec.at[:, 0], vall, loc_sem.at[2]),
    ] + [
        pltpu.make_async_copy(vec.at[mpo * per + v, 0], ext[v].at[1], loc_sem.at[3 + v])
        for v in range(per)
    ]
    for c in local:
        c.start()
    for k in range(nb):
        for c in die_copies(0, k):
            c.start()

    @pl.when(jnp.logical_not(has_behind))
    def _():
        for v in range(per):
            ext[v][slot_fwd] = jnp.zeros(ext[v].shape[1:], BF16)

    pass_tokens()
    acc[...] = jnp.zeros_like(acc)
    for c in local:
        c.wait()

    def share(row, rows, which):
        rows[me] = row[...]

        def send(k, carry):
            other = (me + k) % total
            remote(
                row, rows.at[me], small_s.at[which], small_r.at[which],
                (other // n_mpo, other % n_mpo),
            ).start()
            return carry

        lax.fori_loop(1, total, send, 0)

    def collect(rows, out, which):
        most = rows.at[pl.ds(0, total - 1)]
        pltpu.make_async_copy(most, most, small_s.at[which]).wait()
        pltpu.make_async_copy(most, most, small_r.at[which]).wait()

        def add(k, carry):
            return carry + rows[k]

        line = lax.fori_loop(0, total, add, jnp.zeros(rows.shape[1:], F32)) * scale
        for i in range(nv):
            out[i : i + 1, :] = line[:, i * nv : (i + 1) * nv]

    def forward(v):
        pair_copy(v).wait_recv()

        @pl.when(has_ahead)
        def _():
            fwd_copy(v).start()

    def halo(d, k, c):
        from_chip = (chip + chips - d) % chips
        return 1 + shift[(from_chip * 2 + (core + c) % 2) * nb + k]

    def mid(v, d, k, c):
        return dot(env_l[d, k, c], ext[v][halo(d, k, c)]).astype(BF16)

    def rights(d, k, count):
        block = env_r[d, pl.ds(k, count)]
        return block.reshape(count * 2 * block.shape[2], block.shape[3])

    group = 2 if nb % 2 == 0 else 1

    def near_terms(v):
        @pl.when(has_behind)
        def _():
            fwd_copy(v).wait_recv()

        def step(it, carry):
            mids = [mid(v, 0, it * group + g, c) for g in range(group) for c in range(2)]
            acc[v] += dot(jnp.concatenate(mids, axis=1), rights(0, it * group, group))
            return carry

        lax.fori_loop(0, nb // group, step, 0)

    def far_terms(d, k, last):
        cx = x_copies(d, k)
        cd = die_copies(d, k)
        cx[0].wait_recv()
        cd[0].start()
        first = [mid(v, d, k, 0) for v in range(per)]
        cx[1].wait_recv()
        cd[1].start()
        cd[0].wait_recv()
        second = [mid(v, d, k, 1) for v in range(per)]
        cd[1].wait_recv()
        both = rights(d, k, 1)
        for v in range(per):
            out = acc[v] + dot(jnp.concatenate([first[v], second[v]], axis=1), both)
            if last:
                sigma[v, 0] = out.astype(BF16)
            else:
                acc[v] = out

    forward(0)
    own = jnp.stack([ext[v][1] for v in range(per)], axis=0)
    row_i[...] = gram_row(vall, own, mpo * per, nv, per)
    share(row_i, all_i, 0)
    for k in range(nb):
        for c in die_copies(0, k):
            c.wait_recv()
    for v in range(per):
        if v + 1 < per:
            forward(v + 1)
        near_terms(v)

    for d in range(1, chips):

        def arrive(k, carry):
            far_terms(d, k, False)
            return carry

        lax.fori_loop(0, nb - (d == chips - 1), arrive, 0)
    far_terms(chips - 1, nb - 1, True)
    row_h[...] = gram_row(vall, sigma[:, 0], mpo * per, nv, per)
    share(row_h, all_h, 1)
    collect(all_i, inter, 0)

    for k in range(nb):
        for d in range(chips):
            for c in die_copies(d, k):
                c.wait_send()
            if d:
                for c in x_copies(d, k):
                    c.wait_send()
    for v in range(per):
        pair_copy(v).wait_send()

    @pl.when(has_ahead)
    def _():
        for v in range(per):
            fwd_copy(v).wait_send()

    collect(all_h, ham, 1)


def body(vectors, left_env, right_env, bond_shift):
    n_sec = lax.axis_size("sector")
    n_mpo = lax.axis_size("mpo")
    nv, _, rows, blk = vectors.shape
    nb = left_env.shape[0]
    per = nv // n_mpo
    total = n_sec * n_mpo
    chips = n_mpo // 2
    scale = 1.0 / (n_sec * vectors.shape[1] * rows * blk)
    any_spec = pl.BlockSpec(memory_space=pltpu.HBM)
    vmem_spec = pl.BlockSpec(memory_space=pltpu.VMEM)
    dma = pltpu.SemaphoreType.DMA
    return pl.pallas_call(
        functools.partial(kernel, n_sec, n_mpo, nv, per, nb, scale),
        out_shape=(
            jax.ShapeDtypeStruct((per, 1, rows, blk), BF16),
            jax.ShapeDtypeStruct((nv, nv), F32),
            jax.ShapeDtypeStruct((nv, nv), F32),
        ),
        in_specs=[any_spec] * 3 + [pl.BlockSpec(memory_space=pltpu.SMEM)],
        out_specs=(vmem_spec,) * 3,
        scratch_shapes=[pltpu.VMEM((3, rows, blk), BF16) for _ in range(per)]
        + [
            pltpu.VMEM((chips, nb, 2, rows, rows), BF16),
            pltpu.VMEM((chips, nb, 2, blk, blk), BF16),
            pltpu.VMEM((nv, rows, blk), BF16),
            pltpu.VMEM((per, rows, blk), F32),
            pltpu.VMEM((1, nv * nv), F32),
            pltpu.VMEM((1, nv * nv), F32),
            pltpu.VMEM((total, 1, nv * nv), F32),
            pltpu.VMEM((total, 1, nv * nv), F32),
            dma((3 + per,)),
            dma((per,)), dma((per,)), dma((per,)), dma((per,)),
            dma((chips, 2, nb)), dma((chips, 2, nb)),
            dma((chips, 2, nb)), dma((chips, 2, nb)),
            dma((2,)), dma((2,)),
            pltpu.SemaphoreType.REGULAR((2,)),
        ],
        compiler_params=pltpu.CompilerParams(
            collective_id=0, has_side_effects=True, vmem_limit_bytes=67043328 - (700 << 10)
        ),
        name="davidson",
    )(vectors, left_env, right_env, bond_shift)


def solution(mesh):
    return jax.shard_map(
        body,
        mesh=mesh,
        in_specs=(
            P(None, "sector", None, None),
            P("mpo", "sector", None, None),
            P("mpo", "sector", None, None),
            P(),
        ),
        out_specs=(P("mpo", "sector", None, None), P(), P()),
        check_vma=False,
    )
```

```python
import functools

import jax
import jax.numpy as jnp
from jax import lax
from jax.experimental import pallas as pl
from jax.experimental.pallas import tpu as pltpu
from jax.sharding import PartitionSpec as P

MESH = pl.DeviceIdType.MESH
F32 = jnp.float32
BF16 = jnp.bfloat16


def dot(a, b):
    return jnp.dot(a, b, preferred_element_type=F32)


def gram_row(vall, cols, first, nv, per):
    rows = vall.shape[1]
    blk = vall.shape[2]
    prod = jnp.zeros((per * nv, nv * nv), F32)
    for r in range(rows // nv):
        x = vall[:, r * nv : (r + 1) * nv, :].reshape(nv * nv, blk)
        y = cols[:, r * nv : (r + 1) * nv, :].reshape(per * nv, blk)
        prod += lax.dot_general(y, x, (((1,), (1,)), ((), ())), preferred_element_type=F32)
    sub = lax.broadcasted_iota(jnp.int32, prod.shape, 0) % nv
    lane = lax.broadcasted_iota(jnp.int32, prod.shape, 1) % nv
    prod = jnp.where(sub == lane, prod, 0.0)
    summed = jnp.concatenate(
        [jnp.sum(prod[j * nv : (j + 1) * nv], axis=0, keepdims=True) for j in range(per)], axis=0
    )
    width = nv * nv
    place = lax.broadcasted_iota(jnp.int32, summed.shape, 1) % nv
    step = 1
    while step < nv:
        up = pltpu.roll(summed, step, 1)
        down = pltpu.roll(summed, width - step, 1)
        summed = summed + jnp.where((place // step) % 2 == 1, up, down)
        step *= 2
    which = lax.broadcasted_iota(jnp.int32, summed.shape, 0)
    return jnp.sum(jnp.where(place == first + which, summed, 0.0), axis=0, keepdims=True)


def kernel(n_sec, n_mpo, nv, per, nb, scale, vec, left, right, shift, sigma, inter, ham, *scratch):
    ext = scratch[:per]
    (
        env_l, env_r, vall, acc, row_i, row_h, all_i, all_h,
        loc_sem, pair_s, pair_r, fwd_s, fwd_r, x_s, x_r, die_s, die_r,
        small_s, small_r, token,
    ) = scratch[per:]
    chips = n_mpo // 2
    total = n_sec * n_mpo
    sec = lax.axis_index("sector")
    mpo = lax.axis_index("mpo")
    me = sec * n_mpo + mpo
    core = mpo % 2
    chip = mpo // 2
    partner = chip * 2 + (1 - core)

    par = sec % 2
    pair = sec + 1 - 2 * par
    slot_pair = 2 - 2 * par
    slot_fwd = 2 * par
    ahead = sec + 2 * (1 - 2 * par)
    behind = sec - 2 * (1 - 2 * par)
    has_ahead = (ahead >= 0) & (ahead < n_sec)
    has_behind = (behind >= 0) & (behind < n_sec)

    barrier = pltpu.get_barrier_semaphore()

    def greet(target):
        pl.semaphore_signal(barrier, inc=1, device_id=target, device_id_type=MESH)

    for d in range(1, n_mpo):
        greet((sec, (mpo + d) % n_mpo))
    for d in range(n_mpo):
        greet((pair, (mpo + d) % n_mpo))

    @pl.when(has_ahead)
    def _():
        greet((ahead, mpo))

    @pl.when(has_behind)
    def _():
        greet((behind, mpo))

    pl.semaphore_wait(
        barrier, 2 * n_mpo - 1 + has_ahead.astype(jnp.int32) + has_behind.astype(jnp.int32)
    )

    def pass_tokens():
        @pl.when(has_behind)
        def _():
            pl.semaphore_wait(token.at[0], 1)

        @pl.when(has_ahead)
        def _():
            pl.semaphore_signal(token.at[0], inc=1, device_id=(ahead, mpo), device_id_type=MESH)
            pl.semaphore_wait(token.at[1], 1)

        @pl.when(has_behind)
        def _():
            pl.semaphore_signal(token.at[1], inc=1, device_id=(behind, mpo), device_id_type=MESH)

    def remote(src, dst, send, recv, target):
        return pltpu.make_async_remote_copy(
            src_ref=src, dst_ref=dst, send_sem=send, recv_sem=recv,
            device_id=target, device_id_type=MESH,
        )

    def x_copies(d, k):
        target = (sec, ((chip + d) % chips) * 2 + core)
        return (
            remote(left.at[k, 0], env_l.at[d, k, 0], x_s.at[d, 0, k], x_r.at[d, 0, k], target),
            remote(right.at[k, 0], env_r.at[d, k, 0], x_s.at[d, 1, k], x_r.at[d, 1, k], target),
        )

    def die_copies(d, k):
        target = (sec, partner)
        src_l = left.at[k, 0] if d == 0 else env_l.at[d, k, 0]
        src_r = right.at[k, 0] if d == 0 else env_r.at[d, k, 0]
        return (
            remote(src_l, env_l.at[d, k, 1], die_s.at[d, 0, k], die_r.at[d, 0, k], target),
            remote(src_r, env_r.at[d, k, 1], die_s.at[d, 1, k], die_r.at[d, 1, k], target),
        )

    def pair_copy(v):
        return remote(
            vec.at[mpo * per + v, 0], ext[v].at[slot_fwd], pair_s.at[v], pair_r.at[v], (pair, mpo)
        )

    def fwd_copy(v):
        return remote(
            ext[v].at[slot_pair], ext[v].at[slot_fwd], fwd_s.at[v], fwd_r.at[v], (ahead, mpo)
        )

    for k in range(nb):
        for d in range(1, chips):
            for c in x_copies(d, k):
                c.start()
        if k < per:
            pair_copy(k).start()
    for v in range(nb, per):
        pair_copy(v).start()
    local = [
        pltpu.make_async_copy(left.at[:, 0], env_l.at[0, :, 0], loc_sem.at[0]),
        pltpu.make_async_copy(right.at[:, 0], env_r.at[0, :, 0], loc_sem.at[1]),
        pltpu.make_async_copy(vec.at[:, 0], vall, loc_sem.at[2]),
    ] + [
        pltpu.make_async_copy(vec.at[mpo * per + v, 0], ext[v].at[1], loc_sem.at[3 + v])
        for v in range(per)
    ]
    for c in local:
        c.start()
    for k in range(nb):
        for c in die_copies(0, k):
            c.start()

    @pl.when(jnp.logical_not(has_behind))
    def _():
        for v in range(per):
            ext[v][slot_fwd] = jnp.zeros(ext[v].shape[1:], BF16)

    pass_tokens()
    acc[...] = jnp.zeros_like(acc)
    for c in local:
        c.wait()

    def share(row, rows, which):
        rows[me] = row[...]

        def send(k, carry):
            other = (me + k) % total
            remote(
                row, rows.at[me], small_s.at[which], small_r.at[which],
                (other // n_mpo, other % n_mpo),
            ).start()
            return carry

        lax.fori_loop(1, total, send, 0)

    def collect(rows, out, which):
        most = rows.at[pl.ds(0, total - 1)]
        pltpu.make_async_copy(most, most, small_s.at[which]).wait()
        pltpu.make_async_copy(most, most, small_r.at[which]).wait()

        def add(k, carry):
            return carry + rows[k]

        line = lax.fori_loop(0, total, add, jnp.zeros(rows.shape[1:], F32)) * scale
        for i in range(nv):
            out[i : i + 1, :] = line[:, i * nv : (i + 1) * nv]

    def forward(v):
        pair_copy(v).wait_recv()

        @pl.when(has_ahead)
        def _():
            fwd_copy(v).start()

    def halo(d, k, c):
        from_chip = (chip + chips - d) % chips
        return 1 + shift[(from_chip * 2 + (core + c) % 2) * nb + k]

    def mid(v, d, k, c):
        return dot(env_l[d, k, c], ext[v][halo(d, k, c)]).astype(BF16)

    def rights(d, k, count):
        block = env_r[d, pl.ds(k, count)]
        return block.reshape(count * 2 * block.shape[2], block.shape[3])

    group = 2 if nb % 2 == 0 else 1

    def near_terms(v):
        @pl.when(has_behind)
        def _():
            fwd_copy(v).wait_recv()

        def step(it, carry):
            mids = [mid(v, 0, it * group + g, c) for g in range(group) for c in range(2)]
            acc[v] += dot(jnp.concatenate(mids, axis=1), rights(0, it * group, group))
            return carry

        lax.fori_loop(0, nb // group, step, 0)

    def far_terms(d, k, last):
        cx = x_copies(d, k)
        cd = die_copies(d, k)
        cx[0].wait_recv()
        cd[0].start()
        first = [mid(v, d, k, 0) for v in range(per)]
        cx[1].wait_recv()
        cd[1].start()
        cd[0].wait_recv()
        second = [mid(v, d, k, 1) for v in range(per)]
        cd[1].wait_recv()
        both = rights(d, k, 1)
        for v in range(per):
            out = acc[v] + dot(jnp.concatenate([first[v], second[v]], axis=1), both)
            if last:
                sigma[v, 0] = out.astype(BF16)
            else:
                acc[v] = out

    forward(0)
    own = jnp.stack([ext[v][1] for v in range(per)], axis=0)
    row_i[...] = gram_row(vall, own, mpo * per, nv, per)
    share(row_i, all_i, 0)
    for k in range(nb):
        for c in die_copies(0, k):
            c.wait_recv()
    for v in range(per):
        if v + 1 < per:
            forward(v + 1)
        near_terms(v)

    for d in range(1, chips):

        def arrive(k, carry):
            far_terms(d, k, False)
            return carry

        lax.fori_loop(0, nb - (d == chips - 1), arrive, 0)
    far_terms(chips - 1, nb - 1, True)
    row_h[...] = gram_row(vall, sigma[:, 0], mpo * per, nv, per)
    share(row_h, all_h, 1)
    collect(all_i, inter, 0)

    for k in range(nb):
        for d in range(chips):
            for c in die_copies(d, k):
                c.wait_send()
            if d:
                for c in x_copies(d, k):
                    c.wait_send()
    for v in range(per):
        pair_copy(v).wait_send()

    @pl.when(has_ahead)
    def _():
        for v in range(per):
            fwd_copy(v).wait_send()

    collect(all_h, ham, 1)


def body(vectors, left_env, right_env, bond_shift):
    n_sec = lax.axis_size("sector")
    n_mpo = lax.axis_size("mpo")
    nv, _, rows, blk = vectors.shape
    nb = left_env.shape[0]
    per = nv // n_mpo
    total = n_sec * n_mpo
    chips = n_mpo // 2
    scale = 1.0 / (n_sec * vectors.shape[1] * rows * blk)
    any_spec = pl.BlockSpec(memory_space=pltpu.HBM)
    vmem_spec = pl.BlockSpec(memory_space=pltpu.VMEM)
    dma = pltpu.SemaphoreType.DMA
    return pl.pallas_call(
        functools.partial(kernel, n_sec, n_mpo, nv, per, nb, scale),
        out_shape=(
            jax.ShapeDtypeStruct((per, 1, rows, blk), BF16),
            jax.ShapeDtypeStruct((nv, nv), F32),
            jax.ShapeDtypeStruct((nv, nv), F32),
        ),
        in_specs=[any_spec] * 3 + [pl.BlockSpec(memory_space=pltpu.SMEM)],
        out_specs=(vmem_spec,) * 3,
        scratch_shapes=[pltpu.VMEM((3, rows, blk), BF16) for _ in range(per)]
        + [
            pltpu.VMEM((chips, nb, 2, rows, rows), BF16),
            pltpu.VMEM((chips, nb, 2, blk, blk), BF16),
            pltpu.VMEM((nv, rows, blk), BF16),
            pltpu.VMEM((per, rows, blk), F32),
            pltpu.VMEM((1, nv * nv), F32),
            pltpu.VMEM((1, nv * nv), F32),
            pltpu.VMEM((total, 1, nv * nv), F32),
            pltpu.VMEM((total, 1, nv * nv), F32),
            dma((3 + per,)),
            dma((per,)), dma((per,)), dma((per,)), dma((per,)),
            dma((chips, 2, nb)), dma((chips, 2, nb)),
            dma((chips, 2, nb)), dma((chips, 2, nb)),
            dma((2,)), dma((2,)),
            pltpu.SemaphoreType.REGULAR((2,)),
        ],
        compiler_params=pltpu.CompilerParams(
            collective_id=0, has_side_effects=True, vmem_limit_bytes=52 << 20
        ),
        name="davidson",
    )(*(pltpu.with_memory_space_constraint(x, pltpu.HBM) for x in (vectors, left_env, right_env)), pltpu.with_memory_space_constraint(bond_shift, pltpu.HBM))


def solution(mesh):
    return jax.shard_map(
        body,
        mesh=mesh,
        in_specs=(
            P(None, "sector", None, None),
            P("mpo", "sector", None, None),
            P("mpo", "sector", None, None),
            P(),
        ),
        out_specs=(P("mpo", "sector", None, None), P(), P()),
        check_vma=False,
    )
```

```python
import functools

import jax
import jax.numpy as jnp
from jax import lax
from jax.experimental import pallas as pl
from jax.experimental.pallas import tpu as pltpu
from jax.sharding import PartitionSpec as P

MESH = pl.DeviceIdType.MESH
F32 = jnp.float32
BF16 = jnp.bfloat16


def dot(a, b):
    return jnp.dot(a, b, preferred_element_type=F32)


def gram_row(turned, cols, first, nv, per):
    blk = cols.shape[2]
    prod = jnp.zeros((per * nv, nv * nv), F32)
    for r in range(turned.shape[0]):
        y = cols[:, r * nv : (r + 1) * nv, :].reshape(per * nv, blk)
        prod += dot(y, turned[r])
    sub = lax.broadcasted_iota(jnp.int32, prod.shape, 0) % nv
    lane = lax.broadcasted_iota(jnp.int32, prod.shape, 1) % nv
    prod = jnp.where(sub == lane, prod, 0.0)
    summed = jnp.concatenate(
        [jnp.sum(prod[j * nv : (j + 1) * nv], axis=0, keepdims=True) for j in range(per)], axis=0
    )
    width = nv * nv
    place = lax.broadcasted_iota(jnp.int32, summed.shape, 1) % nv
    step = 1
    while step < nv:
        up = pltpu.roll(summed, step, 1)
        down = pltpu.roll(summed, width - step, 1)
        summed = summed + jnp.where((place // step) % 2 == 1, up, down)
        step *= 2
    which = lax.broadcasted_iota(jnp.int32, summed.shape, 0)
    return jnp.sum(jnp.where(place == first + which, summed, 0.0), axis=0, keepdims=True)


def kernel(n_sec, n_mpo, nv, per, nb, scale, vec, left, right, shift, sigma, inter, ham, *scratch):
    ext = scratch[:per]
    (
        env_l, env_r, vall, turned, acc, row_i, row_h, all_i, all_h,
        loc_sem, pair_s, pair_r, fwd_s, fwd_r, x_s, x_r, die_s, die_r,
        small_s, small_r, token,
    ) = scratch[per:]
    chips = n_mpo // 2
    total = n_sec * n_mpo
    sec = lax.axis_index("sector")
    mpo = lax.axis_index("mpo")
    me = sec * n_mpo + mpo
    core = mpo % 2
    chip = mpo // 2
    partner = chip * 2 + (1 - core)

    par = sec % 2
    pair = sec + 1 - 2 * par
    slot_pair = 2 - 2 * par
    slot_fwd = 2 * par
    ahead = sec + 2 * (1 - 2 * par)
    behind = sec - 2 * (1 - 2 * par)
    has_ahead = (ahead >= 0) & (ahead < n_sec)
    has_behind = (behind >= 0) & (behind < n_sec)

    barrier = pltpu.get_barrier_semaphore()

    def greet(target):
        pl.semaphore_signal(barrier, inc=1, device_id=target, device_id_type=MESH)

    for d in range(1, n_mpo):
        greet((sec, (mpo + d) % n_mpo))
    for d in range(n_mpo):
        greet((pair, (mpo + d) % n_mpo))

    @pl.when(has_ahead)
    def _():
        greet((ahead, mpo))

    @pl.when(has_behind)
    def _():
        greet((behind, mpo))

    pl.semaphore_wait(
        barrier, 2 * n_mpo - 1 + has_ahead.astype(jnp.int32) + has_behind.astype(jnp.int32)
    )

    def pass_tokens():
        @pl.when(has_behind)
        def _():
            pl.semaphore_wait(token.at[0], 1)

        @pl.when(has_ahead)
        def _():
            pl.semaphore_signal(token.at[0], inc=1, device_id=(ahead, mpo), device_id_type=MESH)
            pl.semaphore_wait(token.at[1], 1)

        @pl.when(has_behind)
        def _():
            pl.semaphore_signal(token.at[1], inc=1, device_id=(behind, mpo), device_id_type=MESH)

    def remote(src, dst, send, recv, target):
        return pltpu.make_async_remote_copy(
            src_ref=src, dst_ref=dst, send_sem=send, recv_sem=recv,
            device_id=target, device_id_type=MESH,
        )

    def x_copies(d, k):
        target = (sec, ((chip + d) % chips) * 2 + core)
        return (
            remote(left.at[k, 0], env_l.at[d, k, 0], x_s.at[d, 0, k], x_r.at[d, 0, k], target),
            remote(right.at[k, 0], env_r.at[d, k, 0], x_s.at[d, 1, k], x_r.at[d, 1, k], target),
        )

    def die_copies(d, k):
        target = (sec, partner)
        src_l = left.at[k, 0] if d == 0 else env_l.at[d, k, 0]
        src_r = right.at[k, 0] if d == 0 else env_r.at[d, k, 0]
        return (
            remote(src_l, env_l.at[d, k, 1], die_s.at[d, 0, k], die_r.at[d, 0, k], target),
            remote(src_r, env_r.at[d, k, 1], die_s.at[d, 1, k], die_r.at[d, 1, k], target),
        )

    def pair_copy(v):
        return remote(
            vec.at[mpo * per + v, 0], ext[v].at[slot_fwd], pair_s.at[v], pair_r.at[v], (pair, mpo)
        )

    def fwd_copy(v):
        return remote(
            ext[v].at[slot_pair], ext[v].at[slot_fwd], fwd_s.at[v], fwd_r.at[v], (ahead, mpo)
        )

    for k in range(nb):
        for d in range(1, chips):
            for c in x_copies(d, k):
                c.start()
        if k < per:
            pair_copy(k).start()
    for v in range(nb, per):
        pair_copy(v).start()
    local = [
        pltpu.make_async_copy(left.at[:, 0], env_l.at[0, :, 0], loc_sem.at[0]),
        pltpu.make_async_copy(right.at[:, 0], env_r.at[0, :, 0], loc_sem.at[1]),
        pltpu.make_async_copy(vec.at[:, 0], vall, loc_sem.at[2]),
    ] + [
        pltpu.make_async_copy(vec.at[mpo * per + v, 0], ext[v].at[1], loc_sem.at[3 + v])
        for v in range(per)
    ]
    for c in local:
        c.start()
    for k in range(nb):
        for c in die_copies(0, k):
            c.start()

    @pl.when(jnp.logical_not(has_behind))
    def _():
        for v in range(per):
            ext[v][slot_fwd] = jnp.zeros(ext[v].shape[1:], BF16)

    pass_tokens()
    acc[...] = jnp.zeros_like(acc)
    for c in local:
        c.wait()

    def share(row, rows, which):
        rows[me] = row[...]

        def send(target):
            remote(row, rows.at[me], small_s.at[which], small_r.at[which], target).start()

        def sector(k, carry):
            low = sec < n_sec // 2
            other = jnp.where(low, n_sec - 1 - k, k)
            other = jnp.where(low & (other <= sec), other - 1, other)
            other = jnp.where(jnp.logical_not(low) & (other >= sec), other + 1, other)
            for m in range(n_mpo):
                send((other, m))
            return carry

        lax.fori_loop(0, n_sec - 1, sector, 0)
        for d in range(1, n_mpo):
            send((sec, (mpo + d) % n_mpo))

    def collect(rows, out, which):
        most = rows.at[pl.ds(0, total - 1)]
        pltpu.make_async_copy(most, most, small_s.at[which]).wait()
        pltpu.make_async_copy(most, most, small_r.at[which]).wait()

        line = jnp.sum(rows[...], axis=0) * scale
        for i in range(nv):
            out[i : i + 1, :] = line[:, i * nv : (i + 1) * nv]

    def forward(v):
        pair_copy(v).wait_recv()

        @pl.when(has_ahead)
        def _():
            fwd_copy(v).start()

    def halo(d, k, c):
        from_chip = (chip + chips - d) % chips
        return 1 + shift[(from_chip * 2 + (core + c) % 2) * nb + k]

    def mid(v, d, k, c):
        return dot(env_l[d, k, c], ext[v][halo(d, k, c)]).astype(BF16)

    def rights(d, k, count):
        block = env_r[d, pl.ds(k, count)]
        return block.reshape(count * 2 * block.shape[2], block.shape[3])

    group = 2 if nb % 2 == 0 else 1

    def near_terms(v):
        @pl.when(has_behind)
        def _():
            fwd_copy(v).wait_recv()

        def step(it, carry):
            mids = [mid(v, 0, it * group + g, c) for g in range(group) for c in range(2)]
            acc[v] += dot(jnp.concatenate(mids, axis=1), rights(0, it * group, group))
            return carry

        lax.fori_loop(0, nb // group, step, 0)

    def far_terms(d, k, last):
        cx = x_copies(d, k)
        cd = die_copies(d, k)
        cx[0].wait_recv()
        cd[0].start()
        first = [mid(v, d, k, 0) for v in range(per)]
        cx[1].wait_recv()
        cd[1].start()
        cd[0].wait_recv()
        second = [mid(v, d, k, 1) for v in range(per)]
        cd[1].wait_recv()
        both = rights(d, k, 1)
        for v in range(per):
            out = acc[v] + dot(jnp.concatenate([first[v], second[v]], axis=1), both)
            if last:
                sigma[v, 0] = out.astype(BF16)
            else:
                acc[v] = out

    forward(0)
    own = jnp.stack([ext[v][1] for v in range(per)], axis=0)
    def turn(r, carry):
        x = vall[:, pl.ds(pl.multiple_of(r * nv, nv), nv), :]
        turned[r] = x.reshape(nv * nv, x.shape[2]).T
        return carry

    lax.fori_loop(0, turned.shape[0], turn, 0)
    row_i[...] = gram_row(turned, own, mpo * per, nv, per)
    share(row_i, all_i, 0)
    for k in range(nb):
        for c in die_copies(0, k):
            c.wait_recv()
    for v in range(per):
        if v + 1 < per:
            forward(v + 1)
        near_terms(v)

    for d in range(1, chips):

        def arrive(k, carry):
            far_terms(d, k, False)
            return carry

        lax.fori_loop(0, nb - (d == chips - 1), arrive, 0)
    far_terms(chips - 1, nb - 1, True)
    row_h[...] = gram_row(turned, sigma[:, 0], mpo * per, nv, per)
    share(row_h, all_h, 1)
    collect(all_i, inter, 0)

    for k in range(nb):
        for d in range(chips):
            for c in die_copies(d, k):
                c.wait_send()
            if d:
                for c in x_copies(d, k):
                    c.wait_send()
    for v in range(per):
        pair_copy(v).wait_send()

    @pl.when(has_ahead)
    def _():
        for v in range(per):
            fwd_copy(v).wait_send()

    collect(all_h, ham, 1)


def body(vectors, left_env, right_env, bond_shift):
    n_sec = lax.axis_size("sector")
    n_mpo = lax.axis_size("mpo")
    nv, _, rows, blk = vectors.shape
    nb = left_env.shape[0]
    per = nv // n_mpo
    total = n_sec * n_mpo
    chips = n_mpo // 2
    scale = 1.0 / (n_sec * vectors.shape[1] * rows * blk)
    any_spec = pl.BlockSpec(memory_space=pltpu.HBM)
    vmem_spec = pl.BlockSpec(memory_space=pltpu.VMEM)
    dma = pltpu.SemaphoreType.DMA
    return pl.pallas_call(
        functools.partial(kernel, n_sec, n_mpo, nv, per, nb, scale),
        out_shape=(
            jax.ShapeDtypeStruct((per, 1, rows, blk), BF16),
            jax.ShapeDtypeStruct((nv, nv), F32),
            jax.ShapeDtypeStruct((nv, nv), F32),
        ),
        in_specs=[any_spec] * 3 + [pl.BlockSpec(memory_space=pltpu.SMEM)],
        out_specs=(vmem_spec,) * 3,
        scratch_shapes=[pltpu.VMEM((3, rows, blk), BF16) for _ in range(per)]
        + [
            pltpu.VMEM((chips, nb, 2, rows, rows), BF16),
            pltpu.VMEM((chips, nb, 2, blk, blk), BF16),
            pltpu.VMEM((nv, rows, blk), BF16),
            pltpu.VMEM((rows // nv, blk, nv * nv), BF16),
            pltpu.VMEM((per, rows, blk), F32),
            pltpu.VMEM((1, nv * nv), F32),
            pltpu.VMEM((1, nv * nv), F32),
            pltpu.VMEM((total, 1, nv * nv), F32),
            pltpu.VMEM((total, 1, nv * nv), F32),
            dma((3 + per,)),
            dma((per,)), dma((per,)), dma((per,)), dma((per,)),
            dma((chips, 2, nb)), dma((chips, 2, nb)),
            dma((chips, 2, nb)), dma((chips, 2, nb)),
            dma((2,)), dma((2,)),
            pltpu.SemaphoreType.REGULAR((2,)),
        ],
        compiler_params=pltpu.CompilerParams(
            collective_id=0, has_side_effects=True, vmem_limit_bytes=52 << 20
        ),
        name="davidson",
    )(*(pltpu.with_memory_space_constraint(x, pltpu.HBM) for x in (vectors, left_env, right_env)), pltpu.with_memory_space_constraint(bond_shift, pltpu.HBM))


def solution(mesh):
    return jax.shard_map(
        body,
        mesh=mesh,
        in_specs=(
            P(None, "sector", None, None),
            P("mpo", "sector", None, None),
            P("mpo", "sector", None, None),
            P(),
        ),
        out_specs=(P("mpo", "sector", None, None), P(), P()),
        check_vma=False,
    )
```
